128 devices in a mesh: sta: 16 (over z, y), tile: 8 (over x, core).
Axes of the slice: x: 4, y: 4, z: 4, core: 2. Of those that a mesh axis runs over, the one named last changes fastest.
Arguments:
- traces: bfloat16 [3072, 3072], P('sta', 'tile'), may hold values from -6 to 6
- fir_taps: float32 [4, 64], replicated, may hold values from -0.75 to 0.75
- band_gain: float32 [4], replicated, may hold values from 0.5 to 2
- starts: int32 [3072, 8], P('sta'), may hold values from 0 to 2688
- delays: int32 [3072, 16384], P('sta', 'tile'), may hold values from 0 to 127
- visibility: int32 [3072, 8], P('sta'), may hold values from 0 to 1, as said below
Outputs:
- image: float32 [16384, 256], P(('tile', 'sta'))
The draws below stay inside these ranges and needn't reach their ends.
Inputs may be any that keep to these rules, and one draw needn't show every extreme that they name: `visibility`: 1 where the station contributes to the tile's grid points, else 0; how many stations a tile uses may differ from tile to tile.
All inputs are finite; a program needn't handle non-finite values.
Results may differ from the reference program's by a relative error of at most 0.0051.
Values may be sent and summed in bfloat16 or wider, within the bound.
No kernel may reach another device: no remote copies, remote signals or barrier semaphores. Data moves between devices by JAX's collectives and lax.ppermute only.
A program may use at most 64 MiB of HBM per device.

```python
import math
import jax
import jax.numpy as jnp
from jax import lax

BANDS = 4
TAPS = 64
D = 128
L = 256
G_DEV = 2048
WLEN = 384
TILES = 8
STATIONS = 3072
GRID = 16384
SAMP = 3072


def draw_visibility(key, part):
    first_key, second_key = jax.random.split(jax.random.fold_in(key, 7))
    level = jax.random.randint(first_key, (1, TILES), 1, 5)
    roll = jax.random.randint(second_key, (STATIONS, TILES), 0, 4)
    return (roll < level).astype(jnp.int32)


def plant(values, key, least, high):
    longest = values.shape.index(max(values.shape))
    spots = []
    for shift in (0, 1):
        where = [jax.random.randint(jax.random.fold_in(key, axis), (), 0, length) for axis, length in enumerate(values.shape)]
        where[longest] = (where[longest] + shift) % values.shape[longest]
        spots.append(tuple(where))
    return values.at[spots[0]].set(least).at[spots[1]].set(high)


def level_of(key, dims, pieces, smallest, high):
    def one(position, parts):
        draws = jax.random.uniform(jax.random.fold_in(jax.random.fold_in(key, 6), position), (parts,), jnp.float32, smallest / len(pieces), high / len(pieces))
        return jnp.repeat(jnp.exp(draws), dims[position] // parts).reshape((-1,) + (1,) * (len(dims) - position - 1))

    level = one(*pieces[0])
    for cut in pieces[1:]:
        level = level * one(*cut)
    return level


def noise(stream_key, shape, spread, bound, shards=(), kind=jnp.bfloat16):
    result = jax.random.normal(stream_key, shape, jnp.float32) * spread
    if len(shards) > 0:
        result = level_of(stream_key, shape, shards, -0.22, 0.18) * result
    return jnp.clip(result, min=-bound, max=bound).astype(kind)


def setup_inputs(seed: int = 0) -> dict:
    key_of = jax.random.split(jax.random.key(seed), 7)
    traces = noise(key_of[0], (STATIONS, SAMP), 1.0, 6.0, ((0, 16), (1, 8)))
    fir_taps = noise(key_of[1], (BANDS, TAPS), TAPS ** -0.5, 0.75, (), jnp.float32)
    band_gain = jnp.clip(jnp.exp(jax.random.uniform(key_of[2], (BANDS,), jnp.float32, math.log(0.5), math.log(2.0))), 0.5, 2.0)
    starts = plant(jax.random.randint(key_of[3], (STATIONS, TILES), 0, SAMP - WLEN + 1), jax.random.fold_in(key_of[3], 1), 0, SAMP - WLEN).astype(jnp.int32)
    delays = plant(jax.random.randint(key_of[4], (STATIONS, GRID), 0, D), jax.random.fold_in(key_of[4], 1), 0, D - 1).astype(jnp.int32)
    visibility = draw_visibility(jax.random.fold_in(key_of[6], 71), 0)
    return dict(traces=traces, fir_taps=fir_taps, band_gain=band_gain, starts=starts, delays=delays, visibility=visibility)


def band_filter(extended, fir_taps):
    signal = extended[:, None, :]
    kernel = jnp.flip(fir_taps, 1)[:, None, :]
    return lax.conv_general_dilated(signal, kernel, (1,), 'VALID', dimension_numbers=('NCH', 'OIH', 'NCH'), precision=lax.Precision.HIGHEST)

def character(extended, fir_taps, band_gain):
    filtered = band_filter(extended, fir_taps)
    return lax.optimization_barrier(jnp.sum(filtered * filtered * band_gain[None, :, None], axis=1))

def reference(traces, fir_taps, band_gain, starts, delays, visibility):
    extended = jnp.pad(traces.astype(jnp.float32), ((0, 0), (TAPS - 1, 0)))
    char_fn = character(extended, fir_taps, band_gain).astype(jnp.bfloat16)
    offsets = jnp.arange(WLEN, dtype=jnp.int32)
    sample_idx = starts[:, :, None] + offsets[None, None, :]
    raw_windows = jax.vmap(lambda trace_row, index_set: trace_row[index_set])(char_fn, sample_idx).astype(jnp.float32)
    centred = raw_windows - lax.optimization_barrier(jnp.mean(raw_windows, axis=2, keepdims=True))
    windows = (centred * visibility[:, :, None].astype(jnp.float32)).astype(jnp.bfloat16)
    lag_idx = jnp.arange(D, dtype=jnp.int32)[:, None] + jnp.arange(L, dtype=jnp.int32)[None, :]
    tile_of = jnp.arange(GRID, dtype=jnp.int32) // G_DEV

    def stack_one(total, payload):
        window, delay_row = payload
        hankel = window[:, lag_idx].reshape(TILES * D, L)
        picked_rows = hankel[tile_of * D + delay_row]
        return (total + picked_rows.astype(jnp.float32), None)
    total, unused = lax.scan(stack_one, jnp.zeros((GRID, L), jnp.float32), (windows, delays))
    return total / math.sqrt(STATIONS)
```

```python
import functools
import math

import jax
import jax.numpy as jnp
from jax import lax
from jax.experimental import pallas as pl
from jax.experimental.pallas import tpu as pltpu
from jax.sharding import Mesh, PartitionSpec as P

TAPS = 64
D = 128
L = 256
WLEN = 384
BANDS = 4
LANE = 128
BF16 = jnp.bfloat16
F32 = jnp.float32
VMEM_LIMIT = 60 << 20


def vmem():
    return pl.BlockSpec(memory_space=pltpu.VMEM)


def smem():
    return pl.BlockSpec(memory_space=pltpu.SMEM)


def shift_to(value, axis, by):
    length = lax.axis_size(axis)
    return lax.ppermute(value, axis, [(i, (i + by) % length) for i in range(length)])


def prep_kernel(place, delays, taps, *outs):
    pieces, toeplitz = outs[:-1], outs[-1]
    z = place[0]
    stations, width = delays.shape[0], delays.shape[1] // len(pieces)
    for k, piece in enumerate(pieces):
        chunk = lax.rem(z + k, len(pieces))
        rows = delays[:, pl.ds(pl.multiple_of(chunk * width, LANE), width)].astype(F32)
        columns = jnp.transpose(rows)
        tail = columns[:, LANE:stations]
        piece[:, 0:LANE] = columns[:, 0:LANE].astype(BF16)
        piece[:, LANE : 2 * LANE] = jnp.concatenate([tail, tail - 1.0], axis=1).astype(BF16)
    for b in range(BANDS):
        row = jnp.broadcast_to(taps[b : b + 1, :], (2 * LANE, 2 * LANE))
        band = pltpu.roll(row, 0, axis=1, stride=1, stride_axis=0)[:, 0:LANE]
        for part in range(3):
            rounded = band.astype(BF16)
            toeplitz[part, :, b * LANE : (b + 1) * LANE] = rounded
            band = band - rounded.astype(F32)


def window_kernel(place, gain, mine, other, starts, visibility, toeplitz, out, line):
    x, core = place[2], place[3]
    stations, samp = mine.shape[1], mine.shape[2]
    chips = mine.shape[0]
    tiles_in = (2 * chips * samp) // LANE
    line[:, 0:LANE] = jnp.zeros((stations, LANE), F32)
    line[:, (tiles_in + 1) * LANE :] = jnp.zeros((stations, LANE), F32)
    for k in range(chips):
        chip = lax.rem(x + chips - k, chips)
        for src, c in ((mine, core), (other, 1 - core)):
            at = pl.multiple_of((2 * chip + c) * samp + LANE, LANE)
            line[:, pl.ds(at, samp)] = src[k].astype(F32)
    tile = 2 * x + core
    lane = lax.broadcasted_iota(jnp.int32, starts.shape, 1)
    first = jnp.sum(jnp.where(lane == tile, starts[...], 0), axis=1, keepdims=True) + (LANE - TAPS + 1)
    visible = jnp.sum(jnp.where(lane == tile, visibility[...], 0), axis=1, keepdims=True).astype(F32)
    parts = [line[:, i * LANE : (i + 1) * LANE] for i in range(tiles_in + 2)]
    keep = WLEN // LANE + 2
    bit = 16
    while bit:
        size = min(len(parts), bit - 1 + keep)
        chosen = (first & (bit * LANE)) != 0
        parts = [
            jnp.where(chosen, parts[i + bit], parts[i]) if i + bit < len(parts) else parts[i]
            for i in range(size)
        ]
        bit //= 2
    span = jnp.concatenate(parts, axis=1)
    width = span.shape[1]
    bit = LANE // 2
    while bit:
        chosen = (first & bit) != 0
        span = jnp.where(chosen, pltpu.roll(span, width - bit, axis=1), span)
        bit //= 2
    span = span.astype(BF16)
    blocks = jnp.concatenate([span[:, j * LANE : j * LANE + 2 * LANE] for j in range(WLEN // LANE)], axis=0)
    filtered = sum(jnp.dot(blocks, toeplitz[p], preferred_element_type=F32) for p in range(3))
    char = sum(gain[b] * jnp.square(filtered[:, b * LANE : (b + 1) * LANE]) for b in range(BANDS))
    char = char.astype(BF16).astype(F32)
    char = jnp.concatenate([char[j * stations : (j + 1) * stations] for j in range(WLEN // LANE)], axis=1)
    mean = jnp.sum(char, axis=1, keepdims=True) / WLEN
    out[...] = ((char - mean) * visible).astype(BF16)


def one_hot(column, level):
    return jnp.where(column == jnp.asarray(level, BF16), jnp.asarray(1, BF16), jnp.asarray(0, BF16))


def stack_parts(columns, windows, table):
    w = windows[...]
    for d in range(D):
        rolled = pltpu.roll(w, (WLEN - d) % WLEN, axis=1)[:, 0:L]
        table[d * LANE : (d + 1) * LANE, :] = rolled[0:LANE]
        half = LANE // 2
        table[D * LANE + d * half : D * LANE + (d + 1) * half, :] = rolled[LANE:]
    head, tail = columns[:, 0:LANE], columns[:, LANE : 2 * LANE]
    picks = [one_hot(head, d) for d in range(D)] + [one_hot(tail, d) for d in range(0, D, 2)]
    return jnp.dot(jnp.concatenate(picks, axis=1), table[...], preferred_element_type=F32)


def own_kernel(columns, windows, out, table):
    out[...] = stack_parts(columns, windows, table)


def rest_kernel(place, acc, *refs):
    count = 3
    columns, windows = refs[:count], refs[count : 2 * count]
    kept, sends = refs[2 * count], refs[2 * count + 1 : 2 * count + 4]
    table, total, now_columns, now_windows = refs[2 * count + 4 :]
    step = pl.program_id(0)
    for k in range(count):

        @pl.when(step == k)
        def _():
            now_columns[...] = columns[k][...]
            now_windows[...] = windows[k][...]

    @pl.when(step == 0)
    def _():
        total[...] = acc[...]

    total[...] += stack_parts(now_columns, now_windows, table)

    @pl.when(step == count - 1)
    def _():
        y = place[1]
        rows = kept.shape[0]
        kept[...] = total[pl.ds(pl.multiple_of(y * rows, rows), rows), :]
        for k, send in enumerate(sends):
            at = lax.rem(y + k + 1, 4)
            send[...] = total[pl.ds(pl.multiple_of(at * rows, rows), rows), :].astype(BF16)


def on_device(traces, fir_taps, band_gain, starts, delays, visibility):
    stations, samp = traces.shape
    grid_dev = delays.shape[1]
    piece = grid_dev // 4
    place = jnp.stack([lax.axis_index(a) for a in ("z", "y", "x", "core")]).astype(jnp.int32)
    params = pltpu.CompilerParams(vmem_limit_bytes=VMEM_LIMIT)

    near = [traces] + [shift_to(traces, "x", k) for k in (1, 2, 3)]

    circle = jnp.concatenate(
        [fir_taps[:, TAPS - 1 :], jnp.zeros((BANDS, 2 * LANE - TAPS), F32), fir_taps[:, : TAPS - 1]], axis=1
    )
    prepared = pl.pallas_call(
        prep_kernel,
        out_shape=[jax.ShapeDtypeStruct((piece, 2 * LANE), BF16)] * 4
        + [jax.ShapeDtypeStruct((3, 2 * LANE, BANDS * LANE), BF16)],
        in_specs=[smem(), vmem(), vmem()],
        out_specs=[vmem()] * 5,
        compiler_params=params,
        name="prep",
    )(place, delays, circle)
    own_columns, toeplitz = prepared[0], prepared[4]
    far_columns = [shift_to(prepared[k], "z", k) for k in (1, 2, 3)]

    mine = jnp.stack(near)
    other = shift_to(mine, "core", 1)
    windows = pl.pallas_call(
        window_kernel,
        out_shape=jax.ShapeDtypeStruct((stations, WLEN), BF16),
        in_specs=[smem(), smem()] + [vmem()] * 5,
        out_specs=vmem(),
        scratch_shapes=[pltpu.VMEM((stations, 8 * samp + 2 * LANE), F32)],
        compiler_params=params,
        name="window",
    )(place, band_gain, mine, other, starts, visibility, toeplitz)
    far_windows = [shift_to(windows, "z", k) for k in (1, 2, 3)]

    table = pltpu.VMEM((stations * D, L), BF16)
    flops = 2 * piece * stations * D * L
    own = pl.pallas_call(
        own_kernel,
        out_shape=jax.ShapeDtypeStruct((piece, L), F32),
        in_specs=[vmem()] * 2,
        out_specs=vmem(),
        scratch_shapes=[table],
        compiler_params=params,
        cost_estimate=pl.CostEstimate(flops=flops, bytes_accessed=1 << 20, transcendentals=0),
        name="own",
    )(own_columns, windows)
    rows = piece // 4
    kept, *sends = pl.pallas_call(
        rest_kernel,
        grid=(3,),
        out_shape=[jax.ShapeDtypeStruct((rows, L), F32)] + [jax.ShapeDtypeStruct((rows, L), BF16)] * 3,
        in_specs=[smem()] + [vmem()] * 7,
        out_specs=[vmem()] * 4,
        scratch_shapes=[
            table,
            pltpu.VMEM((piece, L), F32),
            pltpu.VMEM((piece, 2 * LANE), BF16),
            pltpu.VMEM((stations, WLEN), BF16),
        ],
        compiler_params=params,
        cost_estimate=pl.CostEstimate(flops=3 * flops, bytes_accessed=2 << 20, transcendentals=0),
        name="rest",
    )(place, own, *far_columns, *far_windows)
    received = [shift_to(send, "y", k + 1) for k, send in enumerate(sends)]
    total = kept + sum(r.astype(F32) for r in received)
    return total / math.sqrt(stations * 16)


def solution(mesh):
    split = Mesh(mesh.devices.reshape(4, 4, 4, 2), ("z", "y", "x", "core"))
    sta, tile = ("z", "y"), ("x", "core")
    placed = (P(sta, tile), P(), P(), P(sta, None), P(sta, tile), P(sta, None))
    return jax.shard_map(
        on_device, mesh=split, in_specs=placed, out_specs=P(("x", "core", "z", "y"), None), check_vma=False
    )
```

```python
import functools
import math

import jax
import jax.numpy as jnp
from jax import lax
from jax.experimental import pallas as pl
from jax.experimental.pallas import tpu as pltpu
from jax.sharding import Mesh, PartitionSpec as P

TAPS = 64
D = 128
L = 256
WLEN = 384
BANDS = 4
LANE = 128
BF16 = jnp.bfloat16
F32 = jnp.float32
VMEM_LIMIT = 16 << 20


def vmem():
    return pl.BlockSpec(memory_space=pltpu.VMEM)


def smem():
    return pl.BlockSpec(memory_space=pltpu.SMEM)


def shift_to(value, axis, by):
    length = lax.axis_size(axis)
    return lax.ppermute(value, axis, [(i, (i + by) % length) for i in range(length)])


def near_peer(z):
    return z ^ 1


def far_peer(z):
    return 3 - z


def swap(value, peer):
    return lax.ppermute(value, "z", [(i, peer(i)) for i in range(4)])


def as_columns(rows, out):
    columns = jnp.transpose(rows.astype(F32))
    tail = columns[:, LANE:]
    out[:, 0:LANE] = columns[:, 0:LANE].astype(BF16)
    out[:, LANE : 2 * LANE] = jnp.concatenate([tail, tail - 1.0], axis=1).astype(BF16)


def as_lanes(row):
    return jnp.transpose(jnp.broadcast_to(row.astype(F32), (LANE, row.shape[1]))).astype(jnp.int32)


def delay_kernel(delays, own_send, own_keep, peer_both):
    z = lax.axis_index("z")
    width = delays.shape[1] // 4

    def rows_of(chunk):
        return delays[:, pl.ds(pl.multiple_of(chunk * width, LANE), width)]

    peer = near_peer(z)
    for i, chunk in enumerate((far_peer(peer), peer)):
        peer_both[:, i * width : (i + 1) * width] = rows_of(chunk).astype(F32).astype(BF16)
    as_columns(rows_of(far_peer(z)), own_send)
    as_columns(rows_of(z), own_keep)


def band_kernel(taps, starts, visibility, toeplitz, meta, circle):
    circle[...] = jnp.zeros_like(circle)
    circle[0:BANDS, 0:TAPS] = taps[...]
    turned = pltpu.roll(circle[...], 2 * LANE - TAPS + 1, axis=1)
    for b in range(BANDS):
        row = jnp.broadcast_to(turned[b : b + 1, :], (2 * LANE, 2 * LANE))
        band = pltpu.roll(row, 0, axis=1, stride=1, stride_axis=0)[:, 0:LANE]
        for part in range(3):
            rounded = band.astype(BF16)
            toeplitz[part, :, b * LANE : (b + 1) * LANE] = rounded
            band = band - rounded.astype(F32)
    tile = 2 * lax.axis_index("x") + lax.axis_index("core")
    meta[0] = as_lanes(starts[pl.ds(tile, 1), :]) + (LANE - TAPS + 1)
    meta[1] = as_lanes(visibility[pl.ds(tile, 1), :])


def window_kernel(gain, *refs):
    chips = 4
    mine, other = refs[:chips], refs[chips : 2 * chips]
    meta, toeplitz, out, line = refs[2 * chips :]
    x, core = lax.axis_index("x"), lax.axis_index("core")
    stations, samp = mine[0].shape
    tiles_in = (2 * chips * samp) // LANE
    line[:, 0:LANE] = jnp.zeros((stations, LANE), F32)
    line[:, (tiles_in + 1) * LANE :] = jnp.zeros((stations, LANE), F32)
    for k in range(chips):
        chip = lax.rem(x + chips - k, chips)
        for src, c in ((mine, core), (other, 1 - core)):
            at = pl.multiple_of((2 * chip + c) * samp + LANE, LANE)
            line[:, pl.ds(at, samp)] = src[k][...].astype(F32)
    first = meta[0]
    visible = meta[1].astype(F32)
    parts = [line[:, i * LANE : (i + 1) * LANE] for i in range(tiles_in + 2)]
    keep = WLEN // LANE + 2
    bit = 16
    while bit:
        size = min(len(parts), bit - 1 + keep)
        chosen = (first & (bit * LANE)) != 0
        parts = [
            jnp.where(chosen, parts[i + bit], parts[i]) if i + bit < len(parts) else parts[i]
            for i in range(size)
        ]
        bit //= 2
    span = jnp.concatenate(parts, axis=1)
    width = span.shape[1]
    bit = LANE // 2
    while bit:
        chosen = jnp.concatenate([(first & bit)] * (width // LANE), axis=1) != 0
        span = jnp.where(chosen, pltpu.roll(span, width - bit, axis=1), span)
        bit //= 2
    span = span.astype(BF16)
    blocks = jnp.concatenate([span[:, j * LANE : j * LANE + 2 * LANE] for j in range(WLEN // LANE)], axis=0)
    filtered = sum(jnp.dot(blocks, toeplitz[p], preferred_element_type=F32) for p in range(3))
    char = sum(gain[b] * jnp.square(filtered[:, b * LANE : (b + 1) * LANE]) for b in range(BANDS))
    char = char.astype(BF16).astype(F32)
    pieces = [char[j * stations : (j + 1) * stations] for j in range(WLEN // LANE)]
    mean = jnp.sum(sum(pieces), axis=1, keepdims=True) / WLEN
    for j, piece in enumerate(pieces):
        out[:, j * LANE : (j + 1) * LANE] = ((piece - mean) * visible).astype(BF16)


def one_hot(column, level):
    return jnp.where(column == jnp.asarray(level, BF16), jnp.asarray(1, BF16), jnp.asarray(0, BF16))


def fill_table(windows, table):
    w = windows[...]
    half = LANE // 2
    for d in range(D):
        rolled = pltpu.roll(w, (WLEN - d) % WLEN, axis=1)[:, 0:L]
        table[d * LANE : (d + 1) * LANE, :] = rolled[0:LANE]
        table[D * LANE + d * half : D * LANE + (d + 1) * half, :] = rolled[LANE:]


def pick_rows(columns, table):
    head, tail = columns[:, 0:LANE], columns[:, LANE : 2 * LANE]
    picks = [one_hot(head, d) for d in range(D)] + [one_hot(tail, d) for d in range(0, D, 2)]
    return jnp.dot(jnp.concatenate(picks, axis=1), table[...], preferred_element_type=F32)


def own_send_kernel(columns, windows, out, table):
    fill_table(windows, table)
    out[...] = pick_rows(columns, table)


def peer_send_kernel(delay_rows, windows, acc, out, table, keep_columns, columns):
    half = delay_rows.shape[1] // 2
    as_columns(delay_rows[:, 0:half], columns)
    as_columns(delay_rows[:, half:], keep_columns)
    fill_table(windows, table)
    out[...] = (acc[...] + pick_rows(columns, table)).astype(BF16)


def own_keep_kernel(columns, table, out):
    out[...] = pick_rows(columns, table)


def block_at(y, rows):
    return pl.ds(pl.multiple_of(lax.rem(y, 4) * rows, rows), rows)


def peer_keep_kernel(scale, columns, table, acc, received, *sends):
    y = lax.axis_index("y")
    rows = sends[0].shape[0]
    blocks = [block_at(y + k + 1, rows) for k in range(len(sends))]
    picked = pick_rows(jnp.concatenate([columns[b, :] for b in blocks], axis=0), table)
    for k, (b, send) in enumerate(zip(blocks, sends)):
        done = acc[b, :] + received[b, :].astype(F32)
        send[...] = ((done + picked[k * rows : (k + 1) * rows]) * scale).astype(BF16)


def last_kernel(scale, columns, table, acc, received, out):
    rows = out.shape[0]
    b = block_at(lax.axis_index("y"), rows)
    done = acc[b, :] + received[b, :].astype(F32)
    out[...] = (done + pick_rows(columns[b, :], table)) * scale


def cost(flops, size):
    return pl.CostEstimate(flops=flops, bytes_accessed=size, transcendentals=0)


def on_device(traces, fir_taps, band_gain, starts, delays, visibility):
    stations, samp = traces.shape
    piece = delays.shape[1] // 4
    shape = jax.ShapeDtypeStruct
    params = pltpu.CompilerParams(vmem_limit_bytes=VMEM_LIMIT)

    near = [traces] + [shift_to(traces, "x", k) for k in (1, 2, 3)]
    own_send, own_keep, peer_both = pl.pallas_call(
        delay_kernel,
        out_shape=[
            shape((piece, 2 * LANE), BF16),
            shape((piece, 2 * LANE), BF16),
            shape((stations, 2 * piece), BF16),
        ],
        in_specs=[vmem()],
        out_specs=[vmem()] * 3,
        compiler_params=params,
        cost_estimate=cost(1 << 32, 4 << 20),
        name="delay",
    )(delays)
    toeplitz, meta = pl.pallas_call(
        band_kernel,
        out_shape=[shape((3, 2 * LANE, BANDS * LANE), BF16), shape((2, stations, LANE), jnp.int32)],
        in_specs=[vmem()] * 3,
        out_specs=[vmem()] * 2,
        scratch_shapes=[pltpu.VMEM((8, 2 * LANE), F32)],
        compiler_params=params,
        cost_estimate=cost(1 << 31, 1 << 20),
        name="band",
    )(fir_taps, starts.T, visibility.T)
    peer_rows = swap(peer_both, near_peer)
    near, toeplitz, _ = lax.optimization_barrier((near, toeplitz, peer_both))
    other = [shift_to(block, "core", 1) for block in near]

    windows = pl.pallas_call(
        window_kernel,
        out_shape=shape((stations, WLEN), BF16),
        in_specs=[smem()] + [vmem()] * 10,
        out_specs=vmem(),
        scratch_shapes=[pltpu.VMEM((stations, 8 * samp + 2 * LANE), F32)],
        compiler_params=params,
        cost_estimate=cost(1 << 20, 1 << 16),
        name="window",
    )(band_gain, *near, *other, meta, toeplitz)
    peer_windows = swap(windows, near_peer)

    rows = piece // 4
    scale = 1.0 / math.sqrt(stations * 16)
    table = shape((stations * D, L), BF16)
    flat = shape((piece, 2 * LANE), BF16)
    whole, block, rounded = shape((piece, L), F32), shape((rows, L), F32), shape((rows, L), BF16)

    def stack(kernel, name, count, outs, args, scratch=()):
        return pl.pallas_call(
            kernel,
            out_shape=outs,
            in_specs=[vmem()] * len(args),
            out_specs=[vmem()] * len(outs),
            scratch_shapes=list(scratch),
            compiler_params=params,
            cost_estimate=cost(1 << 20, 1 << 16),
            name=name,
        )(*args)

    acc, own_table = stack(own_send_kernel, "own_send", piece, [whole, table], [own_send, windows])
    away, peer_table, peer_keep = stack(
        peer_send_kernel,
        "peer_send",
        piece,
        [shape((piece, L), BF16), table, flat],
        [peer_rows, peer_windows, acc],
        [pltpu.VMEM(flat.shape, flat.dtype)],
    )
    arrived = swap(away, far_peer)
    (acc,) = stack(own_keep_kernel, "own_keep", piece, [whole], [own_keep, own_table])
    args = [peer_keep, peer_table, acc, arrived]
    sends = stack(functools.partial(peer_keep_kernel, scale), "peer_keep", 3 * rows, [rounded] * 3, args)
    (kept,) = stack(functools.partial(last_kernel, scale), "last", rows, [block], args)
    received = [shift_to(send, "y", k + 1) for k, send in enumerate(sends)]
    return kept + sum(r.astype(F32) for r in received)


def solution(mesh):
    split = Mesh(mesh.devices.reshape(4, 4, 4, 2), ("z", "y", "x", "core"))
    sta, tile = ("z", "y"), ("x", "core")
    placed = (P(sta, tile), P(), P(), P(sta, None), P(sta, tile), P(sta, None))
    return jax.shard_map(
        on_device, mesh=split, in_specs=placed, out_specs=P(("x", "core", "z", "y"), None), check_vma=False
    )
```

```python
import functools
import math

import jax
import jax.numpy as jnp
from jax import lax
from jax.experimental import pallas as pl
from jax.experimental.pallas import tpu as pltpu
from jax.sharding import Mesh, PartitionSpec as P

TAPS = 64
HALF = 64
L = 256
WLEN = 384
BANDS = 4
LANE = 128
BF16 = jnp.bfloat16
F32 = jnp.float32
VMEM_LIMIT = 24 << 20


def vmem():
    return pl.BlockSpec(memory_space=pltpu.VMEM)


def smem():
    return pl.BlockSpec(memory_space=pltpu.SMEM)


def shift_to(value, axis, by):
    length = lax.axis_size(axis)
    return lax.ppermute(value, axis, [(i, (i + by) % length) for i in range(length)])


def near_peer(z):
    return z ^ 1


def far_peer(z):
    return 3 - z


def swap(value, peer):
    return lax.ppermute(value, "z", [(i, peer(i)) for i in range(4)])


def as_lanes(row):
    return jnp.transpose(jnp.broadcast_to(row.astype(F32), (LANE, row.shape[1]))).astype(jnp.int32)


def delay_kernel(delays, own_send, own_keep, peer_both):
    z = lax.axis_index("z")
    width = delays.shape[1] // 4

    def rows_of(chunk):
        return delays[:, pl.ds(pl.multiple_of(chunk * width, LANE), width)].astype(F32).astype(BF16)

    peer = near_peer(z)
    peer_both[:, 0:width] = rows_of(far_peer(peer))
    peer_both[:, width : 2 * width] = rows_of(peer)
    own_send[...] = rows_of(far_peer(z))
    own_keep[...] = rows_of(z)


def band_kernel(taps, starts, visibility, toeplitz, meta, circle):
    circle[...] = jnp.zeros_like(circle)
    circle[0:BANDS, 0:TAPS] = taps[...]
    turned = pltpu.roll(circle[...], 2 * LANE - TAPS + 1, axis=1)
    for b in range(BANDS):
        row = jnp.broadcast_to(turned[b : b + 1, :], (2 * LANE, 2 * LANE))
        band = pltpu.roll(row, 0, axis=1, stride=1, stride_axis=0)[:, 0:LANE]
        for part in range(3):
            rounded = band.astype(BF16)
            toeplitz[part, :, b * LANE : (b + 1) * LANE] = rounded
            band = band - rounded.astype(F32)
    tile = 2 * lax.axis_index("x") + lax.axis_index("core")
    meta[0] = as_lanes(starts[pl.ds(tile, 1), :]) + (LANE - TAPS + 1)
    meta[1] = as_lanes(visibility[pl.ds(tile, 1), :])


def window_kernel(gain, *refs):
    chips = 4
    mine, other = refs[:chips], refs[chips : 2 * chips]
    meta, toeplitz, out, line = refs[2 * chips :]
    x, core = lax.axis_index("x"), lax.axis_index("core")
    stations, samp = mine[0].shape
    tiles_in = (2 * chips * samp) // LANE
    line[:, 0:LANE] = jnp.zeros((stations, LANE), F32)
    line[:, (tiles_in + 1) * LANE :] = jnp.zeros((stations, LANE), F32)
    for k in range(chips):
        chip = lax.rem(x + chips - k, chips)
        for src, c in ((mine, core), (other, 1 - core)):
            at = pl.multiple_of((2 * chip + c) * samp + LANE, LANE)
            line[:, pl.ds(at, samp)] = src[k][...].astype(F32)
    first = meta[0]
    visible = meta[1].astype(F32)
    parts = [line[:, i * LANE : (i + 1) * LANE] for i in range(tiles_in + 2)]
    keep = WLEN // LANE + 2
    bit = 16
    while bit:
        size = min(len(parts), bit - 1 + keep)
        chosen = (first & (bit * LANE)) != 0
        parts = [
            jnp.where(chosen, parts[i + bit], parts[i]) if i + bit < len(parts) else parts[i]
            for i in range(size)
        ]
        bit //= 2
    span = jnp.concatenate(parts, axis=1)
    width = span.shape[1]
    bit = LANE // 2
    while bit:
        chosen = jnp.concatenate([(first & bit)] * (width // LANE), axis=1) != 0
        span = jnp.where(chosen, pltpu.roll(span, width - bit, axis=1), span)
        bit //= 2
    span = span.astype(BF16)
    blocks = jnp.concatenate([span[:, j * LANE : j * LANE + 2 * LANE] for j in range(WLEN // LANE)], axis=0)
    filtered = sum(jnp.dot(blocks, toeplitz[p], preferred_element_type=F32) for p in range(3))
    char = sum(gain[b] * jnp.square(filtered[:, b * LANE : (b + 1) * LANE]) for b in range(BANDS))
    char = char.astype(BF16).astype(F32)
    pieces = [char[j * stations : (j + 1) * stations] for j in range(WLEN // LANE)]
    mean = jnp.sum(sum(pieces), axis=1, keepdims=True) / WLEN
    for j, piece in enumerate(pieces):
        out[:, j * LANE : (j + 1) * LANE] = ((piece - mean) * visible).astype(BF16)


def one_hot(delay, level):
    return jnp.where(delay == jnp.asarray(level, BF16), jnp.asarray(1, BF16), jnp.asarray(0, BF16))


def fill_table(windows, table, plain, steps):
    turned = jnp.transpose(windows[...].astype(F32))
    rest = turned[:, LANE:]
    plain[0] = turned[:, 0:LANE]
    plain[1] = jnp.concatenate([rest, pltpu.roll(rest, WLEN - 1, axis=0)], axis=1)
    for i in range(2):
        steps[i] = plain[i, 0 : WLEN - HALF, :] - plain[i, HALF:WLEN, :]
    for part, (source, first) in enumerate(((steps, 0), (plain, HALF), (steps, HALF))):
        for tile in range(HALF + HALF // 2):
            i, d = (0, tile) if tile < HALF else (1, 2 * (tile - HALF))
            for k in range(2):
                at = first + k * 2 * HALF + d
                table[part, k * HALF : (k + 1) * HALF, tile * LANE : (tile + 1) * LANE] = source[
                    i, at : at + HALF, :
                ].astype(BF16)


def pick_rows(delays, table):
    shift = jnp.asarray(HALF, BF16)
    low = jnp.where(delays >= shift, delays - shift, delays)

    def product(part, values, base):
        head, rest = values[0:LANE], values[LANE:]
        rows = [one_hot(head, base + d) for d in range(HALF)] + [one_hot(rest, base + d) for d in range(HALF)]
        return jnp.dot(table[part], jnp.concatenate(rows, axis=0), preferred_element_type=F32)

    first, both, second = product(0, delays, 0), product(1, low, 0), product(2, delays, HALF)
    blocks = []
    for k in range(2):
        here = slice(k * HALF, (k + 1) * HALF)
        blocks += [both[here] + first[here], both[here] - second[here]]
    return jnp.concatenate(blocks, axis=0)


def own_send_kernel(delays, windows, out, table, plain, steps):
    fill_table(windows, table, plain, steps)
    out[...] = pick_rows(delays[...], table)


def peer_send_kernel(delays, windows, acc, out, table, plain, steps):
    fill_table(windows, table, plain, steps)
    half = delays.shape[1] // 2
    out[...] = (acc[...] + pick_rows(delays[:, 0:half], table)).astype(BF16)


def own_keep_kernel(delays, table, out):
    out[...] = pick_rows(delays[...], table)


def peer_keep_kernel(scale, delays, table, acc, received, kept, *rest):
    sends, total = rest[:-1], rest[-1]
    half = delays.shape[1] // 2
    rows = kept.shape[0]
    done = acc[...] + received[...].astype(F32)
    total[...] = (done + pick_rows(delays[:, half:], table)) * scale

    def block(k):
        at = lax.rem(lax.axis_index("y") + k, 4) * rows
        return jnp.transpose(total[:, pl.ds(pl.multiple_of(at, rows), rows)])

    for k, send in enumerate(sends):
        send[...] = block(k + 1).astype(BF16)
    kept[...] = block(0)


def cost(flops, size):
    return pl.CostEstimate(flops=flops, bytes_accessed=size, transcendentals=0)


def on_device(traces, fir_taps, band_gain, starts, delays, visibility):
    stations, samp = traces.shape
    piece = delays.shape[1] // 4
    shape = jax.ShapeDtypeStruct
    params = pltpu.CompilerParams(vmem_limit_bytes=VMEM_LIMIT)

    near = [traces] + [shift_to(traces, "x", k) for k in (1, 2, 3)]
    own_send, own_keep, peer_both = pl.pallas_call(
        delay_kernel,
        out_shape=[
            shape((stations, piece), BF16),
            shape((stations, piece), BF16),
            shape((stations, 2 * piece), BF16),
        ],
        in_specs=[vmem()],
        out_specs=[vmem()] * 3,
        compiler_params=params,
        cost_estimate=cost(1 << 32, 4 << 20),
        name="delay",
    )(delays)
    toeplitz, meta = pl.pallas_call(
        band_kernel,
        out_shape=[shape((3, 2 * LANE, BANDS * LANE), BF16), shape((2, stations, LANE), jnp.int32)],
        in_specs=[vmem()] * 3,
        out_specs=[vmem()] * 2,
        scratch_shapes=[pltpu.VMEM((8, 2 * LANE), F32)],
        compiler_params=params,
        cost_estimate=cost(1 << 31, 1 << 20),
        name="band",
    )(fir_taps, starts.T, visibility.T)
    peer_rows = swap(peer_both, near_peer)
    near, toeplitz, _ = lax.optimization_barrier((near, toeplitz, peer_both))
    other = [shift_to(block, "core", 1) for block in near]

    windows = pl.pallas_call(
        window_kernel,
        out_shape=shape((stations, WLEN), BF16),
        in_specs=[smem()] + [vmem()] * 10,
        out_specs=vmem(),
        scratch_shapes=[pltpu.VMEM((stations, 8 * samp + 2 * LANE), F32)],
        compiler_params=params,
        cost_estimate=cost(1 << 20, 1 << 16),
        name="window",
    )(band_gain, *near, *other, meta, toeplitz)
    peer_windows = swap(windows, near_peer)

    rows = piece // 4
    scale = 1.0 / math.sqrt(stations * 16)
    table = shape((3, LANE, stations * HALF), BF16)
    whole, block, rounded = shape((L, piece), F32), shape((rows, L), F32), shape((rows, L), BF16)
    turned = [pltpu.VMEM((2, WLEN, LANE), F32), pltpu.VMEM((2, WLEN - HALF, LANE), F32)]

    def stack(kernel, name, outs, args, scratch=()):
        return pl.pallas_call(
            kernel,
            out_shape=outs,
            in_specs=[vmem()] * len(args),
            out_specs=[vmem()] * len(outs),
            scratch_shapes=list(scratch),
            compiler_params=params,
            cost_estimate=cost(1 << 20, 1 << 16),
            name=name,
        )(*args)

    acc, own_table = stack(own_send_kernel, "own_send", [whole, table], [own_send, windows], turned)
    away, peer_table = stack(
        peer_send_kernel, "peer_send", [shape((L, piece), BF16), table], [peer_rows, peer_windows, acc], turned
    )
    arrived = swap(away, far_peer)
    (acc,) = stack(own_keep_kernel, "own_keep", [whole], [own_keep, own_table])
    kept, *sends = stack(
        functools.partial(peer_keep_kernel, scale),
        "peer_keep",
        [block] + [rounded] * 3,
        [peer_rows, peer_table, acc, arrived],
        [pltpu.VMEM(whole.shape, F32)],
    )
    received = [shift_to(send, "y", k + 1) for k, send in enumerate(sends)]
    return kept + sum(r.astype(F32) for r in received)


def solution(mesh):
    split = Mesh(mesh.devices.reshape(4, 4, 4, 2), ("z", "y", "x", "core"))
    sta, tile = ("z", "y"), ("x", "core")
    placed = (P(sta, tile), P(), P(), P(sta, None), P(sta, tile), P(sta, None))
    return jax.shard_map(
        on_device, mesh=split, in_specs=placed, out_specs=P(("x", "core", "z", "y"), None), check_vma=False
    )
```

```python
import functools
import math

import jax
import jax.numpy as jnp
from jax import lax
from jax.experimental import pallas as pl
from jax.experimental.pallas import tpu as pltpu
from jax.sharding import Mesh, PartitionSpec as P

TAPS = 64
HALF = 64
L = 256
WLEN = 384
BANDS = 4
LANE = 128
BF16 = jnp.bfloat16
F32 = jnp.float32
VMEM_LIMIT = 24 << 20


def vmem():
    return pl.BlockSpec(memory_space=pltpu.VMEM)


def smem():
    return pl.BlockSpec(memory_space=pltpu.SMEM)


def shift_to(value, axis, by):
    length = lax.axis_size(axis)
    return lax.ppermute(value, axis, [(i, (i + by) % length) for i in range(length)])


def near_peer(i):
    return i ^ 1


def far_peer(i):
    return 3 - i


def swap(value, axis, peer):
    return lax.ppermute(value, axis, [(i, peer(i)) for i in range(4)])


def as_lanes(row):
    return jnp.transpose(jnp.broadcast_to(row.astype(F32), (LANE, row.shape[1]))).astype(jnp.int32)


def delay_kernel(delays, own_send, own_keep, peer_both):
    z = lax.axis_index("z")
    width = delays.shape[1] // 4

    def rows_of(chunk):
        return delays[:, pl.ds(pl.multiple_of(chunk * width, LANE), width)].astype(F32).astype(BF16)

    peer = near_peer(z)
    peer_both[:, 0:width] = rows_of(far_peer(peer))
    peer_both[:, width : 2 * width] = rows_of(peer)
    own_send[...] = rows_of(far_peer(z))
    own_keep[...] = rows_of(z)


def band_kernel(taps, starts, visibility, toeplitz, meta, circle):
    circle[...] = jnp.zeros_like(circle)
    circle[0:BANDS, 0:TAPS] = taps[...]
    turned = pltpu.roll(circle[...], 2 * LANE - TAPS + 1, axis=1)
    for b in range(BANDS):
        row = jnp.broadcast_to(turned[b : b + 1, :], (2 * LANE, 2 * LANE))
        band = pltpu.roll(row, 0, axis=1, stride=1, stride_axis=0)[:, 0:LANE]
        for part in range(3):
            rounded = band.astype(BF16)
            toeplitz[part, :, b * LANE : (b + 1) * LANE] = rounded
            band = band - rounded.astype(F32)
    tile = 2 * lax.axis_index("x") + lax.axis_index("core")
    meta[0] = as_lanes(starts[pl.ds(tile, 1), :]) + (LANE - TAPS + 1)
    meta[1] = as_lanes(visibility[pl.ds(tile, 1), :])


def window_kernel(gain, *refs):
    chips = 4
    mine, other = refs[:chips], refs[chips : 2 * chips]
    meta, toeplitz, out, line = refs[2 * chips :]
    x, core = lax.axis_index("x"), lax.axis_index("core")
    stations, samp = mine[0].shape
    tiles_in = (2 * chips * samp) // LANE
    line[:, 0:LANE] = jnp.zeros((stations, LANE), F32)
    line[:, (tiles_in + 1) * LANE :] = jnp.zeros((stations, LANE), F32)
    for k in range(chips):
        chip = lax.rem(x + chips - k, chips)
        for src, c in ((mine, core), (other, 1 - core)):
            at = pl.multiple_of((2 * chip + c) * samp + LANE, LANE)
            line[:, pl.ds(at, samp)] = src[k][...].astype(F32)
    first = meta[0]
    visible = meta[1].astype(F32)
    parts = [line[:, i * LANE : (i + 1) * LANE] for i in range(tiles_in + 2)]
    keep = WLEN // LANE + 2
    bit = 16
    while bit:
        size = min(len(parts), bit - 1 + keep)
        chosen = (first & (bit * LANE)) != 0
        parts = [
            jnp.where(chosen, parts[i + bit], parts[i]) if i + bit < len(parts) else parts[i]
            for i in range(size)
        ]
        bit //= 2
    span = jnp.concatenate(parts, axis=1)
    width = span.shape[1]
    bit = LANE // 2
    while bit:
        chosen = jnp.concatenate([(first & bit)] * (width // LANE), axis=1) != 0
        span = jnp.where(chosen, pltpu.roll(span, width - bit, axis=1), span)
        bit //= 2
    span = span.astype(BF16)
    blocks = jnp.concatenate([span[:, j * LANE : j * LANE + 2 * LANE] for j in range(WLEN // LANE)], axis=0)
    filtered = sum(jnp.dot(blocks, toeplitz[p], preferred_element_type=F32) for p in range(3))
    char = sum(gain[b] * jnp.square(filtered[:, b * LANE : (b + 1) * LANE]) for b in range(BANDS))
    char = char.astype(BF16).astype(F32)
    pieces = [char[j * stations : (j + 1) * stations] for j in range(WLEN // LANE)]
    mean = jnp.sum(sum(pieces), axis=1, keepdims=True) / WLEN
    for j, piece in enumerate(pieces):
        out[:, j * LANE : (j + 1) * LANE] = ((piece - mean) * visible).astype(BF16)


def one_hot(delay, level):
    return jnp.where(delay == jnp.asarray(level, BF16), jnp.asarray(1, BF16), jnp.asarray(0, BF16))


def fill_table(windows, table, plain, steps):
    turned = jnp.transpose(windows[...].astype(F32))
    rest = turned[:, LANE:]
    plain[0] = turned[:, 0:LANE]
    plain[1] = jnp.concatenate([rest, pltpu.roll(rest, WLEN - 1, axis=0)], axis=1)
    for i in range(2):
        steps[i] = plain[i, 0 : WLEN - HALF, :] - plain[i, HALF:WLEN, :]
    for part, (source, first) in enumerate(((steps, 0), (plain, HALF), (steps, HALF))):
        for tile in range(HALF + HALF // 2):
            i, d = (0, tile) if tile < HALF else (1, 2 * (tile - HALF))
            for k in range(2):
                at = first + k * 2 * HALF + d
                table[part, k * HALF : (k + 1) * HALF, tile * LANE : (tile + 1) * LANE] = source[
                    i, at : at + HALF, :
                ].astype(BF16)


def pick_rows(delays, table):
    shift = jnp.asarray(HALF, BF16)
    low = jnp.where(delays >= shift, delays - shift, delays)

    def product(part, values, base):
        head, rest = values[0:LANE], values[LANE:]
        rows = [one_hot(head, base + d) for d in range(HALF)] + [one_hot(rest, base + d) for d in range(HALF)]
        return jnp.dot(table[part], jnp.concatenate(rows, axis=0), preferred_element_type=F32)

    first, both, second = product(0, delays, 0), product(1, low, 0), product(2, delays, HALF)
    blocks = []
    for k in range(2):
        here = slice(k * HALF, (k + 1) * HALF)
        blocks += [both[here] + first[here], both[here] - second[here]]
    return jnp.concatenate(blocks, axis=0)


def own_send_kernel(delays, windows, out, table, plain, steps):
    fill_table(windows, table, plain, steps)
    out[...] = pick_rows(delays[...], table)


def peer_send_kernel(delays, windows, acc, out, table, plain, steps):
    fill_table(windows, table, plain, steps)
    half = delays.shape[1] // 2
    out[...] = (acc[...] + pick_rows(delays[:, 0:half], table)).astype(BF16)


def y_blocks(ref, *owners):
    rows = ref.shape[1] // 4
    return jnp.concatenate([ref[:, pl.ds(pl.multiple_of(i * rows, rows), rows)] for i in owners], axis=1)


def far_blocks(ref):
    far = far_peer(lax.axis_index("y"))
    return y_blocks(ref, far, near_peer(far))


def near_blocks(ref):
    y = lax.axis_index("y")
    return y_blocks(ref, y, near_peer(y))


def kept_half(ref):
    return ref.at[:, pl.ds(ref.shape[1] // 2, ref.shape[1] // 2)]


def first_keep_kernel(own_delays, own_table, peer_delays, peer_table, far, near, total):
    total[...] = pick_rows(own_delays[...], own_table)
    far[...] = far_blocks(total) + pick_rows(far_blocks(kept_half(peer_delays)), peer_table)
    near[...] = near_blocks(total)


def far_kernel(scale, far, received, out):
    done = (far[...] + far_blocks(received).astype(F32)) * scale
    out[...] = jnp.transpose(done).astype(BF16)


def last_keep_kernel(scale, peer_delays, peer_table, near, received, out):
    done = near[...] + near_blocks(received).astype(F32)
    done = (done + pick_rows(near_blocks(kept_half(peer_delays)), peer_table)) * scale
    out[...] = jnp.transpose(done)


def near_kernel(done, received, kept, send):
    rows = kept.shape[0]
    kept[...] = done[0:rows] + received[0:rows].astype(F32)
    send[...] = (done[rows:] + received[rows:].astype(F32)).astype(BF16)


def cost(flops, size):
    return pl.CostEstimate(flops=flops, bytes_accessed=size, transcendentals=0)


def on_device(traces, fir_taps, band_gain, starts, delays, visibility):
    stations, samp = traces.shape
    piece = delays.shape[1] // 4
    shape = jax.ShapeDtypeStruct
    params = pltpu.CompilerParams(vmem_limit_bytes=VMEM_LIMIT)

    near = [traces] + [shift_to(traces, "x", k) for k in (1, 2, 3)]
    own_send, own_keep, peer_both = pl.pallas_call(
        delay_kernel,
        out_shape=[
            shape((stations, piece), BF16),
            shape((stations, piece), BF16),
            shape((stations, 2 * piece), BF16),
        ],
        in_specs=[vmem()],
        out_specs=[vmem()] * 3,
        compiler_params=params,
        cost_estimate=cost(1 << 32, 4 << 20),
        name="delay",
    )(delays)
    toeplitz, meta = pl.pallas_call(
        band_kernel,
        out_shape=[shape((3, 2 * LANE, BANDS * LANE), BF16), shape((2, stations, LANE), jnp.int32)],
        in_specs=[vmem()] * 3,
        out_specs=[vmem()] * 2,
        scratch_shapes=[pltpu.VMEM((8, 2 * LANE), F32)],
        compiler_params=params,
        cost_estimate=cost(1 << 31, 1 << 20),
        name="band",
    )(fir_taps, starts.T, visibility.T)
    peer_rows = swap(peer_both, "z", near_peer)
    near, toeplitz, _ = lax.optimization_barrier((near, toeplitz, peer_both))
    other = [shift_to(block, "core", 1) for block in near]

    windows = pl.pallas_call(
        window_kernel,
        out_shape=shape((stations, WLEN), BF16),
        in_specs=[smem()] + [vmem()] * 10,
        out_specs=vmem(),
        scratch_shapes=[pltpu.VMEM((stations, 8 * samp + 2 * LANE), F32)],
        compiler_params=params,
        cost_estimate=cost(1 << 20, 1 << 16),
        name="window",
    )(band_gain, *near, *other, meta, toeplitz)
    peer_windows = swap(windows, "z", near_peer)

    rows = piece // 4
    scale = 1.0 / math.sqrt(stations * 16)
    table = shape((3, LANE, stations * HALF), BF16)
    whole, block, rounded = shape((L, piece), F32), shape((rows, L), F32), shape((rows, L), BF16)
    turned = [pltpu.VMEM((2, WLEN, LANE), F32), pltpu.VMEM((2, WLEN - HALF, LANE), F32)]

    def stack(kernel, name, outs, args, scratch=(), flops=1 << 20):
        return pl.pallas_call(
            kernel,
            out_shape=outs,
            in_specs=[vmem()] * len(args),
            out_specs=[vmem()] * len(outs),
            scratch_shapes=list(scratch),
            compiler_params=params,
            cost_estimate=cost(flops, 1 << 16),
            name=name,
        )(*args)

    acc, own_table = stack(own_send_kernel, "own_send", [whole, table], [own_send, windows], turned)
    away, peer_table = stack(
        peer_send_kernel, "peer_send", [shape((L, piece), BF16), table], [peer_rows, peer_windows, acc], turned
    )
    arrived = swap(away, "z", far_peer)
    half = shape((L, 2 * rows), F32)
    far, near_rows = stack(
        first_keep_kernel,
        "first_keep",
        [half, half],
        [own_keep, own_table, peer_rows, peer_table],
        [pltpu.VMEM(whole.shape, F32)],
    )
    (far,) = stack(functools.partial(far_kernel, scale), "far", [shape((2 * rows, L), BF16)], [far, arrived])
    got = swap(far, "y", far_peer)
    near_rows, _ = lax.optimization_barrier((near_rows, far))
    (done,) = stack(
        functools.partial(last_keep_kernel, scale),
        "last_keep",
        [shape((2 * rows, L), F32)],
        [peer_rows, peer_table, near_rows, arrived],
        flops=1 << 32,
    )
    kept, send = stack(near_kernel, "near", [block, rounded], [done, got])
    return kept + swap(send, "y", near_peer).astype(F32)


def solution(mesh):
    split = Mesh(mesh.devices.reshape(4, 4, 4, 2), ("z", "y", "x", "core"))
    sta, tile = ("z", "y"), ("x", "core")
    placed = (P(sta, tile), P(), P(), P(sta, None), P(sta, tile), P(sta, None))
    return jax.shard_map(
        on_device, mesh=split, in_specs=placed, out_specs=P(("x", "core", "z", "y"), None), check_vma=False
    )
```

```python
import functools
import math

import jax
import jax.numpy as jnp
from jax import lax
from jax.experimental import pallas as pl
from jax.experimental.pallas import tpu as pltpu
from jax.sharding import Mesh, PartitionSpec as P

TAPS = 64
HALF = 64
STEP = 24
ROWS = 16
L = 256
WLEN = 384
BANDS = 4
LANE = 128
BF16 = jnp.bfloat16
F32 = jnp.float32
VMEM_LIMIT = 24 << 20


def vmem():
    return pl.BlockSpec(memory_space=pltpu.VMEM)


def smem():
    return pl.BlockSpec(memory_space=pltpu.SMEM)


def shift_to(value, axis, by):
    length = lax.axis_size(axis)
    return lax.ppermute(value, axis, [(i, (i + by) % length) for i in range(length)])


def near_peer(i):
    return i ^ 1


def far_peer(i):
    return 3 - i


def swap(value, axis, peer):
    return lax.ppermute(value, axis, [(i, peer(i)) for i in range(4)])


def as_lanes(row):
    return jnp.transpose(jnp.broadcast_to(row.astype(F32), (LANE, row.shape[1]))).astype(jnp.int32)


def delay_kernel(delays, own_send, own_keep, peer_both):
    z = lax.axis_index("z")
    width = delays.shape[1] // 4

    def rows_of(chunk):
        return delays[:, pl.ds(pl.multiple_of(chunk * width, LANE), width)].astype(F32).astype(BF16)

    peer = near_peer(z)
    peer_both[:, 0:width] = rows_of(far_peer(peer))
    peer_both[:, width : 2 * width] = rows_of(peer)
    own_send[...] = rows_of(far_peer(z))
    own_keep[...] = rows_of(z)


def band_kernel(taps, starts, visibility, toeplitz, meta, circle):
    circle[...] = jnp.zeros_like(circle)
    circle[0:BANDS, 0:TAPS] = taps[...]
    turned = pltpu.roll(circle[...], 2 * LANE - TAPS + 1, axis=1)
    for b in range(BANDS):
        row = jnp.broadcast_to(turned[b : b + 1, :], (2 * LANE, 2 * LANE))
        band = pltpu.roll(row, 0, axis=1, stride=1, stride_axis=0)[:, 0:LANE]
        for part in range(3):
            rounded = band.astype(BF16)
            toeplitz[part, :, b * LANE : (b + 1) * LANE] = rounded
            band = band - rounded.astype(F32)
    tile = 2 * lax.axis_index("x") + lax.axis_index("core")
    meta[0] = as_lanes(starts[pl.ds(tile, 1), :]) + (LANE - TAPS + 1)
    meta[1] = as_lanes(visibility[pl.ds(tile, 1), :])


def window_kernel(gain, *refs):
    chips = 4
    mine, other = refs[:chips], refs[chips : 2 * chips]
    meta, toeplitz, out, line, cut = refs[2 * chips :]
    x, core = lax.axis_index("x"), lax.axis_index("core")
    stations, samp = mine[0].shape
    tiles_in = (2 * chips * samp) // LANE
    line[:, 0:LANE] = jnp.zeros((stations, LANE), BF16)
    line[:, (tiles_in + 1) * LANE :] = jnp.zeros((stations, LANE), BF16)
    for k in range(chips):
        chip = lax.rem(x + chips - k, chips)
        for src, c in ((mine, core), (other, 1 - core)):
            at = pl.multiple_of((2 * chip + c) * samp + LANE, LANE)
            line[:, pl.ds(at, samp)] = src[k][...]
    keep = WLEN // LANE + 2
    for r in range(0, stations, ROWS):
        first = meta[0, r : r + ROWS, :]

        def has(bit):
            return (first & bit).astype(F32).astype(BF16) != jnp.asarray(0, BF16)

        parts = [line[r : r + ROWS, i * LANE : (i + 1) * LANE] for i in range(tiles_in + 2)]
        bit = 16
        while bit:
            size = min(len(parts), bit - 1 + keep)
            chosen = has(bit * LANE)
            parts = [
                jnp.where(chosen, parts[i + bit], parts[i]) if i + bit < len(parts) else parts[i]
                for i in range(size)
            ]
            bit //= 2
        span = jnp.concatenate(parts, axis=1)
        width = span.shape[1]
        bit = LANE // 2
        while bit:
            moved = pltpu.roll(span, width - bit, axis=1)
            chosen = has(bit)
            span = jnp.concatenate(
                [
                    jnp.where(chosen, moved[:, i : i + LANE], span[:, i : i + LANE])
                    for i in range(0, width, LANE)
                ],
                axis=1,
            )
            bit //= 2
        for j in range(WLEN // LANE):
            cut[j * stations + r : j * stations + r + ROWS, :] = span[:, j * LANE : j * LANE + 2 * LANE]
    visible = meta[1].astype(F32)
    blocks = cut[...]
    filtered = sum(jnp.dot(blocks, toeplitz[p], preferred_element_type=F32) for p in range(3))
    char = sum(gain[b] * jnp.square(filtered[:, b * LANE : (b + 1) * LANE]) for b in range(BANDS))
    char = char.astype(BF16).astype(F32)
    pieces = [char[j * stations : (j + 1) * stations] for j in range(WLEN // LANE)]
    mean = jnp.sum(sum(pieces), axis=1, keepdims=True) / WLEN
    for j, piece in enumerate(pieces):
        out[:, j * LANE : (j + 1) * LANE] = ((piece - mean) * visible).astype(BF16)


def one_hot(delay, level):
    return jnp.where(delay == jnp.asarray(level, BF16), jnp.asarray(1, BF16), jnp.asarray(0, BF16))


def turn_windows(windows, plain, steps):
    turned = jnp.transpose(windows[...].astype(F32))
    rest = turned[:, LANE:]
    plain[0] = turned[:, 0:LANE]
    plain[1] = jnp.concatenate([rest, pltpu.roll(rest, WLEN - 1, axis=0)], axis=1)
    for i in range(2):
        steps[i] = plain[i, 0 : WLEN - HALF, :] - plain[i, HALF:WLEN, :]


def fill_tile(source, first, out, tile):
    i, d = (0, tile) if tile < HALF else (1, 2 * (tile - HALF))
    for k in range(2):
        at = first + k * 2 * HALF + d
        out[k * HALF : (k + 1) * HALF, tile * LANE : (tile + 1) * LANE] = source[i, at : at + HALF, :].astype(BF16)


def pick_rows(delays, table, sources=None):
    shift = jnp.asarray(HALF, BF16)
    low = jnp.where(delays >= shift, delays - shift, delays)
    tiles = HALF + HALF // 2
    size = tiles if sources is None else STEP

    def product(part, values, base):
        head, rest = values[0:LANE], values[LANE:]
        total = None
        for begin in range(0, tiles, size):
            rows = []
            for tile in range(begin, begin + size):
                if sources is not None:
                    fill_tile(*sources[part], table.at[part], tile)
                if tile < HALF:
                    rows.append(one_hot(head, base + tile))
                else:
                    d = base + 2 * (tile - HALF)
                    rows += [one_hot(rest, d), one_hot(rest, d + 1)]
            term = jnp.dot(
                table[part, :, begin * LANE : (begin + size) * LANE],
                jnp.concatenate(rows, axis=0),
                preferred_element_type=F32,
            )
            total = term if total is None else total + term
        return total

    first, both, second = product(0, delays, 0), product(1, low, 0), product(2, delays, HALF)
    blocks = []
    for k in range(2):
        here = slice(k * HALF, (k + 1) * HALF)
        blocks += [both[here] + first[here], both[here] - second[here]]
    return jnp.concatenate(blocks, axis=0)


def shifted_sources(plain, steps):
    return (steps, 0), (plain, HALF), (steps, HALF)


def own_send_kernel(delays, windows, out, table, plain, steps):
    turn_windows(windows, plain, steps)
    out[...] = pick_rows(delays[...], table, shifted_sources(plain, steps))


def peer_send_kernel(delays, windows, acc, out, table, plain, steps):
    turn_windows(windows, plain, steps)
    half = delays.shape[1] // 2
    out[...] = (acc[...] + pick_rows(delays[:, 0:half], table, shifted_sources(plain, steps))).astype(BF16)


def y_blocks(ref, *owners):
    rows = ref.shape[1] // 4
    return jnp.concatenate([ref[:, pl.ds(pl.multiple_of(i * rows, rows), rows)] for i in owners], axis=1)


def far_blocks(ref):
    far = far_peer(lax.axis_index("y"))
    return y_blocks(ref, far, near_peer(far))


def near_blocks(ref):
    y = lax.axis_index("y")
    return y_blocks(ref, y, near_peer(y))


def kept_half(ref):
    return ref.at[:, pl.ds(ref.shape[1] // 2, ref.shape[1] // 2)]


def first_keep_kernel(own_delays, own_table, peer_delays, peer_table, far, near, total):
    total[...] = pick_rows(own_delays[...], own_table)
    far[...] = far_blocks(total) + pick_rows(far_blocks(kept_half(peer_delays)), peer_table)
    near[...] = near_blocks(total)


def far_kernel(scale, far, received, out):
    done = (far[...] + far_blocks(received).astype(F32)) * scale
    out[...] = jnp.transpose(done).astype(BF16)


def last_keep_kernel(scale, peer_delays, peer_table, near, received, out):
    done = near[...] + near_blocks(received).astype(F32)
    done = (done + pick_rows(near_blocks(kept_half(peer_delays)), peer_table)) * scale
    out[...] = jnp.transpose(done)


def near_kernel(done, received, kept, send):
    rows = kept.shape[0]
    kept[...] = done[0:rows] + received[0:rows].astype(F32)
    send[...] = (done[rows:] + received[rows:].astype(F32)).astype(BF16)


def cost(flops, size):
    return pl.CostEstimate(flops=flops, bytes_accessed=size, transcendentals=0)


def on_device(traces, fir_taps, band_gain, starts, delays, visibility):
    stations, samp = traces.shape
    piece = delays.shape[1] // 4
    shape = jax.ShapeDtypeStruct
    params = pltpu.CompilerParams(vmem_limit_bytes=VMEM_LIMIT)

    near = [traces] + [shift_to(traces, "x", k) for k in (1, 2, 3)]
    own_send, own_keep, peer_both = pl.pallas_call(
        delay_kernel,
        out_shape=[
            shape((stations, piece), BF16),
            shape((stations, piece), BF16),
            shape((stations, 2 * piece), BF16),
        ],
        in_specs=[vmem()],
        out_specs=[vmem()] * 3,
        compiler_params=params,
        cost_estimate=cost(1 << 32, 4 << 20),
        name="delay",
    )(delays)
    toeplitz, meta = pl.pallas_call(
        band_kernel,
        out_shape=[shape((3, 2 * LANE, BANDS * LANE), BF16), shape((2, stations, LANE), jnp.int32)],
        in_specs=[vmem()] * 3,
        out_specs=[vmem()] * 2,
        scratch_shapes=[pltpu.VMEM((8, 2 * LANE), F32)],
        compiler_params=params,
        cost_estimate=cost(1 << 31, 1 << 20),
        name="band",
    )(fir_taps, starts.T, visibility.T)
    peer_rows = swap(peer_both, "z", near_peer)
    near, toeplitz, _ = lax.optimization_barrier((near, toeplitz, peer_both))
    other = [shift_to(block, "core", 1) for block in near]

    windows = pl.pallas_call(
        window_kernel,
        out_shape=shape((stations, WLEN), BF16),
        in_specs=[smem()] + [vmem()] * 10,
        out_specs=vmem(),
        scratch_shapes=[
            pltpu.VMEM((stations, 8 * samp + 2 * LANE), BF16),
            pltpu.VMEM((WLEN // LANE * stations, 2 * LANE), BF16),
        ],
        compiler_params=params,
        cost_estimate=cost(1 << 20, 1 << 16),
        name="window",
    )(band_gain, *near, *other, meta, toeplitz)
    peer_windows = swap(windows, "z", near_peer)

    rows = piece // 4
    scale = 1.0 / math.sqrt(stations * 16)
    table = shape((3, LANE, stations * HALF), BF16)
    whole, block, rounded = shape((L, piece), F32), shape((rows, L), F32), shape((rows, L), BF16)
    turned = [pltpu.VMEM((2, WLEN, LANE), F32), pltpu.VMEM((2, WLEN - HALF, LANE), F32)]

    def stack(kernel, name, outs, args, scratch=(), flops=1 << 20):
        return pl.pallas_call(
            kernel,
            out_shape=outs,
            in_specs=[vmem()] * len(args),
            out_specs=[vmem()] * len(outs),
            scratch_shapes=list(scratch),
            compiler_params=params,
            cost_estimate=cost(flops, 1 << 16),
            name=name,
        )(*args)

    acc, own_table = stack(own_send_kernel, "own_send", [whole, table], [own_send, windows], turned)
    away, peer_table = stack(
        peer_send_kernel, "peer_send", [shape((L, piece), BF16), table], [peer_rows, peer_windows, acc], turned
    )
    arrived = swap(away, "z", far_peer)
    half = shape((L, 2 * rows), F32)
    far, near_rows = stack(
        first_keep_kernel,
        "first_keep",
        [half, half],
        [own_keep, own_table, peer_rows, peer_table],
        [pltpu.VMEM(whole.shape, F32)],
    )
    (far,) = stack(functools.partial(far_kernel, scale), "far", [shape((2 * rows, L), BF16)], [far, arrived])
    got = swap(far, "y", far_peer)
    near_rows, _ = lax.optimization_barrier((near_rows, far))
    (done,) = stack(
        functools.partial(last_keep_kernel, scale),
        "last_keep",
        [shape((2 * rows, L), F32)],
        [peer_rows, peer_table, near_rows, arrived],
        flops=1 << 32,
    )
    kept, send = stack(near_kernel, "near", [block, rounded], [done, got])
    return kept + swap(send, "y", near_peer).astype(F32)


def solution(mesh):
    split = Mesh(mesh.devices.reshape(4, 4, 4, 2), ("z", "y", "x", "core"))
    sta, tile = ("z", "y"), ("x", "core")
    placed = (P(sta, tile), P(), P(), P(sta, None), P(sta, tile), P(sta, None))
    return jax.shard_map(
        on_device, mesh=split, in_specs=placed, out_specs=P(("x", "core", "z", "y"), None), check_vma=False
    )
```

```python
import functools
import math

import jax
import jax.numpy as jnp
from jax import lax
from jax.experimental import pallas as pl
from jax.experimental.pallas import tpu as pltpu
from jax.sharding import Mesh, PartitionSpec as P

TAPS = 64
HALF = 64
STEP = 24
ROWS = 16
L = 256
WLEN = 384
BANDS = 4
LANE = 128
BF16 = jnp.bfloat16
F32 = jnp.float32
VMEM_LIMIT = 24 << 20


def vmem():
    return pl.BlockSpec(memory_space=pltpu.VMEM)


def smem():
    return pl.BlockSpec(memory_space=pltpu.SMEM)


def shift_to(value, axis, by):
    length = lax.axis_size(axis)
    return lax.ppermute(value, axis, [(i, (i + by) % length) for i in range(length)])


def near_peer(i):
    return i ^ 1


def far_peer(i):
    return 3 - i


def swap(value, axis, peer):
    return lax.ppermute(value, axis, [(i, peer(i)) for i in range(4)])


def as_lanes(row):
    return jnp.transpose(jnp.broadcast_to(row.astype(F32), (LANE, row.shape[1]))).astype(jnp.int32)


def delay_kernel(delays, own_send, own_keep, peer_both):
    z = lax.axis_index("z")
    width = delays.shape[1] // 4

    def rows_of(chunk):
        return delays[:, pl.ds(pl.multiple_of(chunk * width, LANE), width)].astype(F32).astype(BF16)

    peer = near_peer(z)
    peer_both[:, 0:width] = rows_of(far_peer(peer))
    peer_both[:, width : 2 * width] = rows_of(peer)
    own_send[...] = rows_of(far_peer(z))
    own_keep[...] = rows_of(z)


def band_kernel(taps, starts, visibility, toeplitz, meta, circle):
    circle[...] = jnp.zeros_like(circle)
    circle[0:BANDS, 0:TAPS] = taps[...]
    turned = pltpu.roll(circle[...], 2 * LANE - TAPS + 1, axis=1)
    for b in range(BANDS):
        row = jnp.broadcast_to(turned[b : b + 1, :], (2 * LANE, 2 * LANE))
        band = pltpu.roll(row, 0, axis=1, stride=1, stride_axis=0)[:, 0:LANE]
        for part in range(3):
            rounded = band.astype(BF16)
            toeplitz[part, :, b * LANE : (b + 1) * LANE] = rounded
            band = band - rounded.astype(F32)
    tile = 2 * lax.axis_index("x") + lax.axis_index("core")
    meta[0] = as_lanes(starts[pl.ds(tile, 1), :]) + (LANE - TAPS + 1)
    meta[1] = as_lanes(visibility[pl.ds(tile, 1), :])


def window_kernel(gain, *refs):
    chips = 4
    mine, other = refs[:chips], refs[chips : 2 * chips]
    meta, toeplitz, out, turned, line, cut = refs[2 * chips :]
    x, core = lax.axis_index("x"), lax.axis_index("core")
    stations, samp = mine[0].shape
    tiles_in = (2 * chips * samp) // LANE
    line[:, 0:LANE] = jnp.zeros((stations, LANE), BF16)
    line[:, (tiles_in + 1) * LANE :] = jnp.zeros((stations, LANE), BF16)
    for k in range(chips):
        chip = lax.rem(x + chips - k, chips)
        for src, c in ((mine, core), (other, 1 - core)):
            at = pl.multiple_of((2 * chip + c) * samp + LANE, LANE)
            line[:, pl.ds(at, samp)] = src[k][...]
    keep = WLEN // LANE + 2
    for r in range(0, stations, ROWS):
        first = meta[0, r : r + ROWS, :]

        def has(bit):
            return (first & bit).astype(F32).astype(BF16) != jnp.asarray(0, BF16)

        parts = [line[r : r + ROWS, i * LANE : (i + 1) * LANE] for i in range(tiles_in + 2)]
        bit = 16
        while bit:
            size = min(len(parts), bit - 1 + keep)
            chosen = has(bit * LANE)
            parts = [
                jnp.where(chosen, parts[i + bit], parts[i]) if i + bit < len(parts) else parts[i]
                for i in range(size)
            ]
            bit //= 2
        span = jnp.concatenate(parts, axis=1)
        width = span.shape[1]
        bit = LANE // 2
        while bit:
            moved = pltpu.roll(span, width - bit, axis=1)
            chosen = has(bit)
            span = jnp.concatenate(
                [
                    jnp.where(chosen, moved[:, i : i + LANE], span[:, i : i + LANE])
                    for i in range(0, width, LANE)
                ],
                axis=1,
            )
            bit //= 2
        for j in range(WLEN // LANE):
            cut[j * stations + r : j * stations + r + ROWS, :] = span[:, j * LANE : j * LANE + 2 * LANE]
    visible = meta[1].astype(F32)
    blocks = cut[...]
    filtered = sum(jnp.dot(blocks, toeplitz[p], preferred_element_type=F32) for p in range(3))
    char = sum(gain[b] * jnp.square(filtered[:, b * LANE : (b + 1) * LANE]) for b in range(BANDS))
    char = char.astype(BF16).astype(F32)
    pieces = [char[j * stations : (j + 1) * stations] for j in range(WLEN // LANE)]
    mean = jnp.sum(sum(pieces), axis=1, keepdims=True) / WLEN
    centred = jnp.concatenate([(piece - mean) * visible for piece in pieces], axis=1).astype(BF16)
    out[...] = centred
    turn_rows(centred, turned)


def one_hot(delay, level):
    return jnp.where(delay == jnp.asarray(level, BF16), jnp.asarray(1, BF16), jnp.asarray(0, BF16))


def turn_rows(windows, plain):
    turned = jnp.transpose(windows.astype(F32))
    rest = turned[:, LANE:]
    plain[0] = turned[:, 0:LANE]
    plain[1] = jnp.concatenate([rest, pltpu.roll(rest, WLEN - 1, axis=0)], axis=1)


def difference(plain, steps):
    for i in range(2):
        steps[i] = plain[i, 0 : WLEN - HALF, :] - plain[i, HALF:WLEN, :]


def fill_tile(source, first, out, tile):
    i, d = (0, tile) if tile < HALF else (1, 2 * (tile - HALF))
    for k in range(2):
        at = first + k * 2 * HALF + d
        out[k * HALF : (k + 1) * HALF, tile * LANE : (tile + 1) * LANE] = source[i, at : at + HALF, :].astype(BF16)


def pick_rows(delays, table, sources=None):
    shift = jnp.asarray(HALF, BF16)
    low = jnp.where(delays >= shift, delays - shift, delays)
    tiles = HALF + HALF // 2
    size = tiles if sources is None else STEP

    def product(part, values, base):
        head, rest = values[0:LANE], values[LANE:]
        total = None
        for begin in range(0, tiles, size):
            rows = []
            for tile in range(begin, begin + size):
                if sources is not None:
                    fill_tile(*sources[part], table.at[part], tile)
                if tile < HALF:
                    rows.append(one_hot(head, base + tile))
                else:
                    d = base + 2 * (tile - HALF)
                    rows += [one_hot(rest, d), one_hot(rest, d + 1)]
            term = jnp.dot(
                table[part, :, begin * LANE : (begin + size) * LANE],
                jnp.concatenate(rows, axis=0),
                preferred_element_type=F32,
            )
            total = term if total is None else total + term
        return total

    first, both, second = product(0, delays, 0), product(1, low, 0), product(2, delays, HALF)
    blocks = []
    for k in range(2):
        here = slice(k * HALF, (k + 1) * HALF)
        blocks += [both[here] + first[here], both[here] - second[here]]
    return jnp.concatenate(blocks, axis=0)


def shifted_sources(plain, steps):
    return (steps, 0), (plain, HALF), (steps, HALF)


def own_send_kernel(delays, plain, out, table, steps):
    difference(plain, steps)
    out[...] = pick_rows(delays[...], table, shifted_sources(plain, steps))


def peer_send_kernel(delays, windows, acc, out, table, plain, steps):
    turn_rows(windows[...], plain)
    difference(plain, steps)
    half = delays.shape[1] // 2
    out[...] = (acc[...] + pick_rows(delays[:, 0:half], table, shifted_sources(plain, steps))).astype(BF16)


def y_blocks(ref, *owners):
    rows = ref.shape[1] // 4
    return jnp.concatenate([ref[:, pl.ds(pl.multiple_of(i * rows, rows), rows)] for i in owners], axis=1)


def far_blocks(ref):
    far = far_peer(lax.axis_index("y"))
    return y_blocks(ref, far, near_peer(far))


def near_blocks(ref):
    y = lax.axis_index("y")
    return y_blocks(ref, y, near_peer(y))


def kept_half(ref):
    return ref.at[:, pl.ds(ref.shape[1] // 2, ref.shape[1] // 2)]


def first_keep_kernel(own_delays, own_table, peer_delays, peer_table, far, near, total):
    total[...] = pick_rows(own_delays[...], own_table)
    far[...] = far_blocks(total) + pick_rows(far_blocks(kept_half(peer_delays)), peer_table)
    near[...] = near_blocks(total)


def far_kernel(scale, far, received, out):
    done = (far[...] + far_blocks(received).astype(F32)) * scale
    out[...] = jnp.transpose(done).astype(BF16)


def last_keep_kernel(scale, peer_delays, peer_table, near, received, out):
    done = near[...] + near_blocks(received).astype(F32)
    done = (done + pick_rows(near_blocks(kept_half(peer_delays)), peer_table)) * scale
    out[...] = jnp.transpose(done)


def near_kernel(done, received, kept, send):
    rows = kept.shape[0]
    kept[...] = done[0:rows] + received[0:rows].astype(F32)
    send[...] = (done[rows:] + received[rows:].astype(F32)).astype(BF16)


def cost(flops, size):
    return pl.CostEstimate(flops=flops, bytes_accessed=size, transcendentals=0)


def on_device(traces, fir_taps, band_gain, starts, delays, visibility):
    stations, samp = traces.shape
    piece = delays.shape[1] // 4
    shape = jax.ShapeDtypeStruct
    params = pltpu.CompilerParams(vmem_limit_bytes=VMEM_LIMIT)

    near = [traces] + [shift_to(traces, "x", k) for k in (1, 2, 3)]
    own_send, own_keep, peer_both = pl.pallas_call(
        delay_kernel,
        out_shape=[
            shape((stations, piece), BF16),
            shape((stations, piece), BF16),
            shape((stations, 2 * piece), BF16),
        ],
        in_specs=[vmem()],
        out_specs=[vmem()] * 3,
        compiler_params=params,
        cost_estimate=cost(1 << 32, 4 << 20),
        name="delay",
    )(delays)
    toeplitz, meta = pl.pallas_call(
        band_kernel,
        out_shape=[shape((3, 2 * LANE, BANDS * LANE), BF16), shape((2, stations, LANE), jnp.int32)],
        in_specs=[vmem()] * 3,
        out_specs=[vmem()] * 2,
        scratch_shapes=[pltpu.VMEM((8, 2 * LANE), F32)],
        compiler_params=params,
        cost_estimate=cost(1 << 31, 1 << 20),
        name="band",
    )(fir_taps, starts.T, visibility.T)
    peer_rows = swap(peer_both, "z", near_peer)
    near, toeplitz, _ = lax.optimization_barrier((near, toeplitz, peer_both))
    other = [shift_to(block, "core", 1) for block in near]

    windows, own_turned = pl.pallas_call(
        window_kernel,
        out_shape=[shape((stations, WLEN), BF16), shape((2, WLEN, LANE), F32)],
        in_specs=[smem()] + [vmem()] * 10,
        out_specs=[vmem()] * 2,
        scratch_shapes=[
            pltpu.VMEM((stations, 8 * samp + 2 * LANE), BF16),
            pltpu.VMEM((WLEN // LANE * stations, 2 * LANE), BF16),
        ],
        compiler_params=params,
        cost_estimate=cost(1 << 20, 1 << 16),
        name="window",
    )(band_gain, *near, *other, meta, toeplitz)
    peer_windows = swap(windows, "z", near_peer)

    rows = piece // 4
    scale = 1.0 / math.sqrt(stations * 16)
    table = shape((3, LANE, stations * HALF), BF16)
    whole, block, rounded = shape((L, piece), F32), shape((rows, L), F32), shape((rows, L), BF16)
    turned = [pltpu.VMEM((2, WLEN, LANE), F32), pltpu.VMEM((2, WLEN - HALF, LANE), F32)]

    def stack(kernel, name, outs, args, scratch=(), flops=1 << 20):
        return pl.pallas_call(
            kernel,
            out_shape=outs,
            in_specs=[vmem()] * len(args),
            out_specs=[vmem()] * len(outs),
            scratch_shapes=list(scratch),
            compiler_params=params,
            cost_estimate=cost(flops, 1 << 16),
            name=name,
        )(*args)

    acc, own_table = stack(own_send_kernel, "own_send", [whole, table], [own_send, own_turned], turned[1:])
    away, peer_table = stack(
        peer_send_kernel, "peer_send", [shape((L, piece), BF16), table], [peer_rows, peer_windows, acc], turned
    )
    arrived = swap(away, "z", far_peer)
    half = shape((L, 2 * rows), F32)
    far, near_rows = stack(
        first_keep_kernel,
        "first_keep",
        [half, half],
        [own_keep, own_table, peer_rows, peer_table],
        [pltpu.VMEM(whole.shape, F32)],
    )
    (far,) = stack(functools.partial(far_kernel, scale), "far", [shape((2 * rows, L), BF16)], [far, arrived])
    got = swap(far, "y", far_peer)
    near_rows, _ = lax.optimization_barrier((near_rows, far))
    (done,) = stack(
        functools.partial(last_keep_kernel, scale),
        "last_keep",
        [shape((2 * rows, L), F32)],
        [peer_rows, peer_table, near_rows, arrived],
        flops=1 << 32,
    )
    kept, send = stack(near_kernel, "near", [block, rounded], [done, got])
    return kept + swap(send, "y", near_peer).astype(F32)


def solution(mesh):
    split = Mesh(mesh.devices.reshape(4, 4, 4, 2), ("z", "y", "x", "core"))
    sta, tile = ("z", "y"), ("x", "core")
    placed = (P(sta, tile), P(), P(), P(sta, None), P(sta, tile), P(sta, None))
    return jax.shard_map(
        on_device, mesh=split, in_specs=placed, out_specs=P(("x", "core", "z", "y"), None), check_vma=False
    )
```
